32 devices in a mesh: gx: 2 (over y), gy: 4 (over x, core), gz: 4 (over z).
Axes of the slice: x: 2, y: 2, z: 4, core: 2. Of those that a mesh axis runs over, the one named last changes fastest.
Arguments:
- positions: float32 [3, 8, 16, 512], P(None, 'gx', 'gy', 'gz'), may hold values from 0 to 1
- charges: float32 [8, 16, 512], P('gx', 'gy', 'gz'), may hold values from -1.2 to 1.2
- counts: int32 [8, 16, 16], P('gx', 'gy', 'gz'), may hold values from 16 to 32
- moment_shift: bfloat16 [8, 81, 81], replicated, may hold values from -0.25 to 0.25
- far_operators: bfloat16 [81, 25600], replicated, may hold values from -0.046875 to 0.046875
- local_shift: bfloat16 [8, 81, 81], replicated, may hold values from -0.625 to 0.625
- lattice_operator: bfloat16 [81, 81], replicated, may hold values from -0.625 to 0.625
Outputs:
- potential: float32 [8, 16, 512], P('gx', 'gy', 'gz')
- electric_field: float32 [3, 8, 16, 512], P(None, 'gx', 'gy', 'gz')
The draws below stay inside these ranges and needn't reach their ends.
Inputs may be any that keep to these rules, and one draw needn't show every extreme that they name: `counts`: number of live charges in each leaf; slots at or past it are pads.
All inputs are finite; a program needn't handle non-finite values.
Results may differ from the reference program's by a relative error of at most 0.00035.
Values sent between devices are 32-bit elements; how exact they have to be, the bound alone decides.
A program may use at most 256 MiB of HBM per device.

```python
import jax
import jax.numpy as jnp
import numpy as np
from jax import lax

ORDER = 8
TERMS = 81
SLOTS = 32
OPERATOR_COLUMNS = 25600
GRID_X = 8
GRID_Y = 16
GRID_Z = 16


def touch_ends(entries, own_key, least, top_value):
    shape = entries.shape
    spot = [jax.random.randint(jax.random.fold_in(own_key, axis), (), 0, shape[axis]) for axis in range(len(shape))]
    entries = entries.at[tuple(spot)].set(least)
    longest = shape.index(max(shape))
    spot[longest] = (spot[longest] + 1) % shape[longest]
    return entries.at[tuple(spot)].set(top_value)


def block_levels(own_key, dims, shards, least, top_value):
    gain = 1.0
    for axis_at, blocks in shards:
        steps = jax.random.uniform(jax.random.fold_in(jax.random.fold_in(own_key, 6), axis_at), (blocks,), jnp.float32, least / len(shards), top_value / len(shards))
        gain = gain * jnp.repeat(jnp.exp(steps), dims[axis_at] // blocks).reshape((-1,) + (1,) * (len(dims) - 1 - axis_at))
    return gain


def bell_draw(rng, shape, deviation, most, split=(), kind=jnp.bfloat16):
    drawn = jax.random.normal(rng, shape, jnp.float32) * deviation
    if len(split) > 0:
        drawn = block_levels(rng, shape, split, -0.22, 0.18) * drawn
    return jnp.clip(drawn, min=-most, max=most).astype(kind)


def setup_inputs(seed: int = 0) -> dict:
    seeds = jax.random.split(jax.random.key(seed), 8)
    return {
        "positions": jnp.clip(1.0 * jax.random.uniform(seeds[0], (3, GRID_X, GRID_Y, GRID_Z * SLOTS), jnp.float32) ** block_levels(seeds[0], (3, GRID_X, GRID_Y, GRID_Z * SLOTS), ((1, 2), (2, 4), (3, 4)), -0.2, 0.2), 0.0, 1.0),
        "charges": bell_draw(seeds[1], (GRID_X, GRID_Y, GRID_Z * SLOTS), 0.2, 1.2, ((0, 2), (1, 4), (2, 4)), jnp.float32),
        "counts": touch_ends(jax.random.randint(seeds[2], (GRID_X, GRID_Y, GRID_Z), SLOTS // 2, SLOTS + 1), jax.random.fold_in(seeds[2], 1), SLOTS // 2, SLOTS).astype(jnp.int32),
        "moment_shift": bell_draw(seeds[3], (8, TERMS, TERMS), (8 * TERMS) ** -0.5, 0.25),
        "far_operators": bell_draw(seeds[4], (TERMS, OPERATOR_COLUMNS), (189 * TERMS) ** -0.5, 0.046875),
        "local_shift": bell_draw(seeds[5], (8, TERMS, TERMS), TERMS ** -0.5, 0.625),
        "lattice_operator": bell_draw(seeds[6], (TERMS, TERMS), TERMS ** -0.5, 0.625),
    }


SOFTENING = 0.0625

def offset_table():
    listed = []
    for shift_x in range(-3, 4):
        for shift_y in range(-3, 4):
            for shift_z in range(-3, 4):
                if max(abs(shift_x), abs(shift_y), abs(shift_z)) >= 2:
                    listed.append((shift_x, shift_y, shift_z))
    return np.array(listed, dtype=np.int32)

def exponent_table(degree):
    listed = []
    for accumulated in range(degree + 1):
        for height in (0, 1):
            for power_x in range(accumulated - height + 1):
                listed.append((power_x, accumulated - height - power_x, height))
    return np.array(listed, dtype=np.int32)

def power_stack(values, degree):
    listed = [jnp.ones_like(values)]
    for exponent in range(degree):
        listed.append(listed[-1] * values)
    return jnp.stack(listed)

def slope_stack(powers, degree):
    listed = [jnp.zeros_like(powers[0])]
    for exponent in range(1, degree + 1):
        listed.append(float(exponent) * powers[exponent - 1])
    return jnp.stack(listed)

def monomials(relative, degree, with_slopes):
    centred = relative - 0.5
    exponents = exponent_table(degree)
    powers_x = power_stack(centred[0], degree)
    powers_y = power_stack(centred[1], degree)
    powers_z = power_stack(centred[2], degree)
    part_x = powers_x[exponents[:, 0]]
    part_y = powers_y[exponents[:, 1]]
    part_z = powers_z[exponents[:, 2]]
    values = part_x * part_y * part_z
    if not with_slopes:
        return (values, None)
    slope_x = slope_stack(powers_x, degree)[exponents[:, 0]]
    slope_y = slope_stack(powers_y, degree)[exponents[:, 1]]
    slope_z = slope_stack(powers_z, degree)[exponents[:, 2]]
    slopes = (slope_x * part_y * part_z, part_x * slope_y * part_z, part_x * part_y * slope_z)
    return (values, slopes)

def to_moments(stacked):
    values = monomials(stacked[:3], ORDER, False)[0]
    return lax.optimization_barrier(jnp.sum(values * stacked[3][None], axis=-1))

def moments_up(child, operators):
    term_count, size_x, size_y, size_z = child.shape
    grouped = child.reshape(term_count, size_x // 2, 2, size_y // 2, 2, size_z // 2, 2)
    accumulated = jnp.zeros((term_count, size_x // 2 * (size_y // 2) * (size_z // 2)), jnp.float32)
    for octant in range(8):
        child_piece = grouped[:, :, octant >> 2 & 1, :, octant >> 1 & 1, :, octant & 1].reshape(term_count, -1)
        accumulated = accumulated + jnp.dot(operators[octant], child_piece, precision=lax.Precision.HIGHEST)
    return accumulated.reshape(term_count, size_x // 2, size_y // 2, size_z // 2)

def locals_down(parent, operators):
    term_count, size_x, size_y, size_z = parent.shape
    flat_parent = parent.reshape(term_count, -1)
    pieces = [jnp.dot(operators[octant], flat_parent, precision=lax.Precision.HIGHEST).reshape(term_count, size_x, size_y, size_z) for octant in range(8)]
    stacked = jnp.stack(pieces, axis=1).reshape(term_count, 2, 2, 2, size_x, size_y, size_z)
    return stacked.transpose(0, 4, 1, 5, 2, 6, 3).reshape(term_count, 2 * size_x, 2 * size_y, 2 * size_z)

def far_terms(source, grid_shape, coords, parity, operators):
    shifts = offset_table()
    offset_count = shifts.shape[0]
    term_count = source.shape[0]
    shift_x = jnp.asarray(shifts[:, 0:1])
    shift_y = jnp.asarray(shifts[:, 1:2])
    shift_z = jnp.asarray(shifts[:, 2:3])
    size_x, size_y, size_z = grid_shape
    coord_x, coord_y, coord_z = coords
    flat_index = ((coord_x[None, :] + shift_x) % size_x * size_y + (coord_y[None, :] + shift_y) % size_y) * size_z + (coord_z[None, :] + shift_z) % size_z
    picked = jnp.take(source, flat_index, axis=1)
    if parity is not None:
        odd_x, odd_y, odd_z = parity
        admitted = (shift_x >= -2 - odd_x[None, :]) & (shift_x <= 3 - odd_x[None, :])
        admitted = admitted & (shift_y >= -2 - odd_y[None, :]) & (shift_y <= 3 - odd_y[None, :])
        admitted = admitted & (shift_z >= -2 - odd_z[None, :]) & (shift_z <= 3 - odd_z[None, :])
        picked = picked * admitted.astype(jnp.float32)[None]
    ordered = jnp.transpose(picked, (1, 0, 2)).reshape(offset_count * term_count, -1)
    return jnp.dot(operators[:, :offset_count * term_count], ordered, precision=lax.Precision.HIGHEST)

def level_terms(moments, restrict, operators):
    term_count, size_x, size_y, size_z = moments.shape
    target_count = size_x * size_y * size_z
    block_size = min(target_count, 512)
    blocks = jnp.arange(target_count, dtype=jnp.int32).reshape(target_count // block_size, block_size)
    source = moments.reshape(term_count, target_count)

    def one_block(block_rows):
        coord_x = block_rows // (size_y * size_z)
        coord_y = block_rows // size_z % size_y
        coord_z = block_rows % size_z
        parity = (coord_x % 2, coord_y % 2, coord_z % 2) if restrict else None
        return far_terms(source, (size_x, size_y, size_z), (coord_x, coord_y, coord_z), parity, operators)
    result = lax.map(one_block, blocks)
    return result.transpose(1, 0, 2).reshape(term_count, size_x, size_y, size_z)

def evaluate(extended, slab_local, live_mask):
    term_count, size_x, size_y, size_z = slab_local.shape
    slot_count = extended.shape[4]
    target = extended[:, 1:size_x + 1, 1:size_y + 1, 1:size_z + 1, :]
    self_mask = (1.0 - jnp.eye(slot_count, dtype=jnp.float32))[:, None, None, None, :]
    near_potential = jnp.zeros((size_x, size_y, size_z, slot_count), jnp.float32)
    near_x = jnp.zeros_like(near_potential)
    near_y = jnp.zeros_like(near_potential)
    near_z = jnp.zeros_like(near_potential)
    for shift_x in (-1, 0, 1):
        for shift_y in (-1, 0, 1):
            for shift_z in (-1, 0, 1):
                source = extended[:, 1 + shift_x:1 + shift_x + size_x, 1 + shift_y:1 + shift_y + size_y, 1 + shift_z:1 + shift_z + size_z, :]
                source = jnp.moveaxis(source, 4, 1)[..., None]
                delta_x = target[0][None] - source[0] - float(shift_x)
                delta_y = target[1][None] - source[1] - float(shift_y)
                delta_z = target[2][None] - source[2] - float(shift_z)
                distance = delta_x * delta_x + delta_y * delta_y + delta_z * delta_z + SOFTENING
                inverse = lax.rsqrt(distance)
                weight = source[3] * inverse
                if shift_x == 0 and shift_y == 0 and (shift_z == 0):
                    weight = weight * self_mask
                near_potential = near_potential + lax.optimization_barrier(jnp.sum(weight, axis=0))
                cubic_weight = weight * inverse * inverse
                near_x = near_x + lax.optimization_barrier(jnp.sum(cubic_weight * delta_x, axis=0))
                near_y = near_y + lax.optimization_barrier(jnp.sum(cubic_weight * delta_y, axis=0))
                near_z = near_z + lax.optimization_barrier(jnp.sum(cubic_weight * delta_z, axis=0))
    values, slopes = monomials(target[:3], ORDER, True)
    expanded = slab_local[..., None]
    potential = (near_potential + lax.optimization_barrier(jnp.sum(expanded * values, axis=0))) * live_mask
    field_out = jnp.stack([near_x - lax.optimization_barrier(jnp.sum(expanded * slopes[0], axis=0)), near_y - lax.optimization_barrier(jnp.sum(expanded * slopes[1], axis=0)), near_z - lax.optimization_barrier(jnp.sum(expanded * slopes[2], axis=0))]) * live_mask[None]
    return (potential, field_out)

def reference(positions, charges, counts, moment_shift, far_operators, local_shift, lattice_operator):
    slots_index = jnp.arange(SLOTS, dtype=jnp.int32)
    live_mask = (slots_index[None, None, None, :] < counts[..., None]).astype(jnp.float32)
    weights = charges.reshape(GRID_X, GRID_Y, GRID_Z, SLOTS) * live_mask
    stacked = jnp.concatenate([positions.reshape(3, GRID_X, GRID_Y, GRID_Z, SLOTS), weights[None]], axis=0)
    upward = moment_shift.astype(jnp.float32)
    across = far_operators.astype(jnp.float32)
    downward = local_shift.astype(jnp.float32)
    lattice = lattice_operator.astype(jnp.float32)
    moments_leaf = jnp.moveaxis(lax.map(to_moments, jnp.moveaxis(stacked, 1, 0)), 0, 1)
    moments_mid = moments_up(moments_leaf, upward)
    moments_upper = moments_up(moments_mid, upward)
    moments_top = moments_up(moments_upper, upward)
    term_count = moments_top.shape[0]
    root_moments = lax.optimization_barrier(jnp.sum(moments_top.reshape(term_count, -1), axis=1))
    lattice_term = jnp.dot(lattice, root_moments[:, None], precision=lax.Precision.HIGHEST).reshape(term_count, 1, 1, 1)
    local_top = 0.125 * (level_terms(moments_top, False, across) + lattice_term)
    local_upper = 0.25 * level_terms(moments_upper, True, across) + locals_down(local_top, downward)
    local_mid = 0.5 * level_terms(moments_mid, True, across) + locals_down(local_upper, downward)
    local_leaf = level_terms(moments_leaf, True, across) + locals_down(local_mid, downward)
    padded = jnp.pad(stacked, ((0, 0), (1, 1), (1, 1), (1, 1), (0, 0)), mode='wrap')

    def one_slab(slab_row):
        extended = lax.dynamic_slice_in_dim(padded, slab_row, 3, axis=1)
        slab_local = lax.dynamic_slice_in_dim(local_leaf, slab_row, 1, axis=1)
        slab_live = lax.dynamic_slice_in_dim(live_mask, slab_row, 1, axis=0)
        return evaluate(extended, slab_local, slab_live)
    potential, field_out = lax.map(one_slab, jnp.arange(GRID_X, dtype=jnp.int32))
    potential = potential.reshape(GRID_X, GRID_Y, GRID_Z * SLOTS)
    field_out = jnp.moveaxis(field_out, 0, 1).reshape(3, GRID_X, GRID_Y, GRID_Z * SLOTS)
    return (potential, field_out)
```

```python
import jax
import jax.numpy as jnp
import numpy as np
from jax import lax
from jax.experimental import pallas as pl
from jax.experimental.pallas import tpu as pltpu
from jax.sharding import PartitionSpec as P

ORDER = 8
SLOTS = 32


SOFTENING = 0.0625


def padded(cells, sides, width):
    for axis, dim in sides:
        count = lax.axis_size(axis)
        head = lax.slice_in_dim(cells, 0, width, axis=dim)
        tail = lax.slice_in_dim(cells, cells.shape[dim] - width, cells.shape[dim], axis=dim)
        cells = jnp.concatenate(
            [
                lax.ppermute(tail, axis, [(i, (i + 1) % count) for i in range(count)]),
                cells,
                lax.ppermute(head, axis, [((i + 1) % count, i) for i in range(count)]),
            ],
            axis=dim,
        )
    return cells


def offset_table():
    listed = []
    for shift_x in range(-3, 4):
        for shift_y in range(-3, 4):
            for shift_z in range(-3, 4):
                if max(abs(shift_x), abs(shift_y), abs(shift_z)) >= 2:
                    listed.append((shift_x, shift_y, shift_z))
    return np.array(listed, dtype=np.int32)


def exponent_table(degree):
    listed = []
    for accumulated in range(degree + 1):
        for height in (0, 1):
            for power_x in range(accumulated - height + 1):
                listed.append((power_x, accumulated - height - power_x, height))
    return np.array(listed, dtype=np.int32)


NT = (((1,), (1,)), ((), ()))
TN = (((0,), (0,)), ((), ()))
F32 = jnp.float32
BF16 = jnp.bfloat16
LANES = 128


def split_rows(data):
    upper = data.astype(BF16)
    lower = (data - upper.astype(F32)).astype(BF16)
    return upper, lower


def apply(data, operator):
    upper, lower = split_rows(data)
    return lax.dot_general(upper, operator, NT, preferred_element_type=F32) + lax.dot_general(
        lower, operator, NT, preferred_element_type=F32
    )


def exact(left, right, dims):
    return lax.dot_general(
        left, right, dims, precision=lax.Precision.HIGHEST, preferred_element_type=F32
    )


def permutation(block_x, block_y, block_z):
    half_x, half_y, half_z = (block_x // 2, block_y // 2, block_z // 2)
    number = block_x * block_y * block_z
    table = np.zeros((number, number), np.float32)
    for x in range(block_x):
        for y in range(block_y):
            for z in range(block_z):
                octant = 4 * (x % 2) + 2 * (y % 2) + z % 2
                parent = (x // 2 * half_y + y // 2) * half_z + z // 2
                table[octant * (number // 8) + parent, (x * block_y + y) * block_z + z] = 1.0
    return table


def powers_of(values):
    listed = [jnp.ones_like(values)]
    for exponent in range(ORDER):
        listed.append(listed[-1] * values)
    return listed


def monomial_map(powers_x, powers_y, centred_z):
    made = {}
    for power_x, power_y, power_z in exponent_table(ORDER):
        key = (int(power_x), int(power_y), int(power_z))
        if key[2] == 0:
            made[key] = powers_x[key[0]] * powers_y[key[1]]
        else:
            made[key] = made[(key[0], key[1], 0)] * centred_z
    return made


def cell_picker(rows, cells):
    row = lax.broadcasted_iota(jnp.int32, (rows, cells * SLOTS), 0)
    lane = lax.broadcasted_iota(jnp.int32, (rows, cells * SLOTS), 1)
    return (lane // SLOTS == row).astype(F32)


def moment_kernel(cells, data_ref, shift_ref, order_ref, leaf_ref, mid_ref, upper_ref, table):
    terms = shift_ref.shape[1]
    columns = data_ref.shape[1]
    padded_terms = table.shape[0] // columns - 1
    powers_x = powers_of(data_ref[0] - 0.5)
    powers_x = [value * data_ref[3] for value in powers_x]
    powers_y = powers_of(data_ref[1] - 0.5)
    made = monomial_map(powers_x, powers_y, data_ref[2] - 0.5)
    for row, key in enumerate(exponent_table(ORDER)):
        table[row * columns : (row + 1) * columns, :] = made[tuple(int(v) for v in key)]
    spare = (padded_terms + 1 - terms) * columns
    table[terms * columns :, :] = jnp.zeros((spare, table.shape[1]), F32)
    picker = cell_picker(8, cells)
    leaf_ref[...] = jnp.zeros(leaf_ref.shape, F32)
    for column in range(columns):
        rows = table[pl.ds(column, padded_terms, stride=columns), :]
        found = exact(picker, rows, NT)
        leaf_ref[column * cells : (column + 1) * cells, :padded_terms] = found[:cells]
    ordered = exact(order_ref[...], leaf_ref[...], (((1,), (0,)), ((), ())))
    parents = ordered.shape[0] // 8
    mid = jnp.zeros((parents, terms), F32)
    for octant in range(8):
        piece = ordered[octant * parents : (octant + 1) * parents, :terms]
        mid = mid + apply(piece, shift_ref[octant])
    mid_ref[...] = jnp.zeros(mid_ref.shape, F32)
    mid_ref[:, :terms] = mid
    up = jnp.zeros((8, terms), F32)
    for octant in range(8):
        piece = jnp.broadcast_to(mid[octant : octant + 1], (8, terms))
        up = up + apply(piece, shift_ref[octant])
    upper_ref[...] = jnp.zeros(upper_ref.shape, F32)
    upper_ref[:, :terms] = up


def field_kernel(
    sizes,
    tops,
    plan_ref,
    where_ref,
    near_ref,
    live_ref,
    leaf_ref,
    mid_ref,
    upper_ref,
    root_ref,
    far_ref,
    down_ref,
    lattice_ref,
    order_ref,
    potential_ref,
    field_ref,
    spread,
    leaf_rows,
    mid_rows,
    operators,
    top_local,
    local_table,
    sums,
):
    block_x, block_y, block_z = sizes
    columns = block_x * block_y
    width = block_z * SLOTS
    terms = down_ref.shape[1]
    offsets = plan_ref.shape[0] // 16
    padded_terms = operators.shape[1]

    def fill(x, carry):
        for component in range(4):
            for move_z in range(3):
                for move_y in range(3):
                    spread[
                        (component * 3 + move_z) * 3 + move_y, pl.ds(x * block_y, block_y), :
                    ] = near_ref[
                        component, x, move_y : move_y + block_y, move_z * SLOTS : move_z * SLOTS + width
                    ]
        return carry

    lax.fori_loop(0, block_x + 2, fill, 0)

    def place(row, carry):
        start = row * terms
        base = jnp.minimum(start // LANES * LANES, far_ref.shape[1] - 2 * LANES)
        base = pl.multiple_of(base, LANES)
        held = far_ref[:, pl.ds(base, 2 * LANES)].astype(F32)
        held = jnp.concatenate(
            [held, jnp.zeros((padded_terms - terms, 2 * LANES), F32)], axis=0
        )
        turned = pltpu.roll(held, lax.rem(2 * LANES - (start - base), 2 * LANES), 1)
        return turned[:, :LANES].astype(BF16)

    def place_pair(pair, carry):
        operators[pair, :, :LANES] = place(2 * pair, carry)
        operators[pair, :, LANES:] = place(2 * pair + 1, carry)
        return carry

    lax.fori_loop(0, offsets // 2, place_pair, 0, unroll=2)

    lane = lax.broadcasted_iota(jnp.int32, (columns, width), 1)
    group = lane - lane % SLOTS
    turns = [group + (lane + step) % SLOTS for step in range(1, 5)]
    target_x = near_ref_target(near_ref, 0, sizes)
    target_y = near_ref_target(near_ref, 1, sizes)
    target_z = near_ref_target(near_ref, 2, sizes)

    def neighbour(which, totals):
        move_x = which // 9
        move_yz = which % 9
        move_y = move_yz // 3
        move_z = move_yz % 3
        slab = move_z * 3 + move_y
        rows = pl.ds(move_x * block_y, columns)
        shift_x = (move_x - 1).astype(F32)
        shift_y = (move_y - 1).astype(F32)
        shift_z = (move_z - 1).astype(F32)
        source = (
            spread[slab, rows, :] + shift_x,
            spread[9 + slab, rows, :] + shift_y,
            spread[18 + slab, rows, :] + shift_z,
            spread[27 + slab, rows, :],
        )
        own = which == 13

        def step(at, carry):
            held, totals = carry
            keep = jnp.where(own & (at == 0), 0.0, 1.0)
            sum_p, sum_x, sum_y, sum_z = totals
            for turn in range(4):
                if turn == 0:
                    s_x, s_y, s_z, s_q = held
                    s_q = s_q * keep
                else:
                    s_x, s_y, s_z, s_q = [
                        jnp.take_along_axis(value, turns[turn - 1], axis=1) for value in held
                    ]
                d_x = target_x - s_x
                d_y = target_y - s_y
                d_z = target_z - s_z
                inverse = lax.rsqrt(d_x * d_x + d_y * d_y + d_z * d_z + SOFTENING)
                weight = s_q * inverse
                sum_p = sum_p + weight
                cubic = weight * (inverse * inverse)
                sum_x = sum_x + cubic * d_x
                sum_y = sum_y + cubic * d_y
                sum_z = sum_z + cubic * d_z
            held = tuple(jnp.take_along_axis(value, turns[3], axis=1) for value in held)
            return held, (sum_p, sum_x, sum_y, sum_z)

        return lax.fori_loop(0, SLOTS // 4, step, (source, totals))[1]

    zero = jnp.zeros((columns, width), F32)
    near = lax.fori_loop(0, 27, neighbour, (zero, zero, zero, zero))

    row_of = lax.broadcasted_iota(jnp.int32, (8, LANES), 0)

    def sheets(held, cells, move):
        turned = pltpu.roll(held, (8 - (move + 2)) % 8, 0)
        if move == 3:
            turned = jnp.where(row_of % 2 == 0, turned, 0.0)
        if move == -3:
            turned = jnp.where(row_of % 2 == 1, turned, 0.0)
        upper = turned.astype(BF16).astype(F32)
        lower = pltpu.roll(turned - upper, cells, 0)
        made = jnp.where(row_of < cells, upper, lower)
        return jnp.where(row_of < 2 * cells, made, 0.0)

    wide_x, wide_y = leaf_ref.shape[0], leaf_ref.shape[1]
    leaf_rows[...] = jnp.zeros(leaf_rows.shape, F32)
    mid_rows[...] = jnp.zeros(mid_rows.shape, F32)

    def leaf_sheet(at, carry):
        x = at // wide_y
        y = at % wide_y
        held = leaf_ref[x, y]
        for move in range(-3, 4):
            leaf_rows[move + 3, x, y] = sheets(held, block_z, move)
        return carry

    lax.fori_loop(0, wide_x * wide_y, leaf_sheet, 0)
    mid_x, mid_y = mid_ref.shape[0], mid_ref.shape[1]

    def mid_sheet(at, carry):
        x = at // mid_y
        y = at % mid_y
        held = mid_ref[x, y]
        for move in range(-3, 4):
            mid_rows[move + 3, x, y] = sheets(held, block_z // 2, move)
        return carry

    lax.fori_loop(0, mid_x * mid_y, mid_sheet, 0)

    half_x, half_y = block_x // 2, block_y // 2
    upper_rows = upper_ref.shape[1]

    def gathered(row):
        at = row * 16
        move_z = plan_ref[at + 2]
        pieces = []
        for x in range(block_x):
            for y in range(block_y):
                pieces.append(leaf_rows[move_z, plan_ref[at + 4 + x % 2] + x, plan_ref[at + 6 + y % 2] + y])
        for x in range(half_x):
            for y in range(half_y):
                pieces.append(mid_rows[move_z, plan_ref[at + 8 + x % 2] + x, plan_ref[at + 10 + y % 2] + y])
        pieces.append(upper_ref[row, :, :LANES])
        pieces.append(upper_ref[row, :, LANES:])
        return jnp.concatenate(pieces, axis=0).astype(BF16)

    def far_step(pair, total):
        left = jnp.concatenate([gathered(2 * pair), gathered(2 * pair + 1)], axis=1)
        return total + lax.dot_general(left, operators[pair], NT, preferred_element_type=F32)

    leaf_count = columns * 8
    mid_count = half_x * half_y * 8
    total_rows = leaf_count + mid_count + 2 * upper_rows
    sums[...] = lax.fori_loop(
        0, offsets // 2, far_step, jnp.zeros((total_rows, padded_terms), F32), unroll=2
    )
    first = leaf_count + mid_count
    far_high = sums[first : first + upper_rows, :terms] + sums[first + upper_rows :, :terms]
    lattice = apply(jnp.broadcast_to(root_ref[...], (8, root_ref.shape[1]))[:, :terms], lattice_ref[...])
    top_local[...] = 0.125 * (far_high + lattice[:1])
    parent = top_local[pl.ds(where_ref[0] + 1, 1), :]
    upper = 0.25 * far_high[:1] + apply(jnp.broadcast_to(parent, (8, terms)), down_ref[where_ref[1]])[:1]
    upper = jnp.broadcast_to(upper, (8, terms))
    half_z = block_z // 2
    mids = jnp.concatenate([apply(upper, down_ref[octant])[:1] for octant in range(8)], axis=0)
    far_mids = []
    for column in range(half_x * half_y):
        held = sums[leaf_count + column * 8 : leaf_count + column * 8 + 8, :terms]
        far_mids.append(held[:half_z] + held[half_z : 2 * half_z])
    mids = mids + 0.5 * jnp.concatenate(far_mids, axis=0)
    pieces = [apply(mids, down_ref[octant]) for octant in range(8)]
    downs = exact(order_ref[...], jnp.concatenate(pieces, axis=0), TN)
    picker = cell_picker(block_z, block_z)
    for column in range(columns):
        held = sums[column * 8 : column * 8 + 8, :terms]
        local = held[:block_z] + held[block_z : 2 * block_z]
        local = local + downs[column * block_z : (column + 1) * block_z]
        local_table[pl.ds(column, terms, stride=columns), :] = exact(local, picker, TN)

    made = monomial_map(powers_of(target_x - 0.5), powers_of(target_y - 0.5), target_z - 0.5)
    out_p, out_x, out_y, out_z = near
    for row, key in enumerate(exponent_table(ORDER)):
        power_x, power_y, power_z = [int(v) for v in key]
        local = local_table[row * columns : (row + 1) * columns, :]
        out_p = out_p + local * made[(power_x, power_y, power_z)]
        if power_x:
            out_x = out_x - (float(power_x) * local) * made[(power_x - 1, power_y, power_z)]
        if power_y:
            out_y = out_y - (float(power_y) * local) * made[(power_x, power_y - 1, power_z)]
        if power_z:
            out_z = out_z - local * made[(power_x, power_y, 0)]
    live = live_ref[...]
    potential_ref[...] = out_p * live
    field_ref[0] = out_x * live
    field_ref[1] = out_y * live
    field_ref[2] = out_z * live


def near_ref_target(near_ref, component, sizes):
    block_x, block_y, block_z = sizes
    width = block_z * SLOTS
    return jnp.concatenate(
        [near_ref[component, 1 + x, 1 : 1 + block_y, SLOTS : SLOTS + width] for x in range(block_x)],
        axis=0,
    )


def plan_table(block_x, block_y):
    shifts = offset_table()
    plan = np.zeros((shifts.shape[0], 16), np.int32)
    for row, shift in enumerate(shifts):
        for axis in range(3):
            plan[row, axis] = shift[axis] + 3
        for axis in range(2):
            block = (block_x, block_y)[axis]
            for odd in range(2):
                admitted = -2 - odd <= shift[axis] <= 3 - odd
                plan[row, 4 + 2 * axis + odd] = shift[axis] + 2 if admitted else block + 4
                plan[row, 8 + 2 * axis + odd] = shift[axis] + 2 if admitted else block // 2 + 4
    return plan.reshape(-1)


def moments_merge(child, operators):
    size_x, size_y, size_z, terms = child.shape
    grouped = child.reshape(size_x // 2, 2, size_y // 2, 2, size_z // 2, 2, terms)
    grouped = grouped.transpose(0, 2, 4, 1, 3, 5, 6).reshape(-1, 8, terms)
    return jnp.einsum("pok,oak->pa", grouped, operators, precision=lax.Precision.HIGHEST)


def per_device(
    positions, charges, counts, moment_shift, far_operators, local_shift, lattice_operator
):
    block_x, block_y, column = charges.shape
    block_z = column // SLOTS
    sizes = (block_x, block_y, block_z)
    number_x = lax.axis_size("gx")
    number_y = lax.axis_size("gy")
    number_z = lax.axis_size("gz")
    index_x = lax.axis_index("gx")
    index_y = lax.axis_index("gy")
    index_z = lax.axis_index("gz")
    terms = moment_shift.shape[1]
    padded_terms = (terms + 15) // 16 * 16
    columns = block_x * block_y
    leaves = columns * block_z
    slot_of = jnp.arange(column, dtype=jnp.int32) % SLOTS
    live_mask = (slot_of[None, None, :] < jnp.repeat(counts, SLOTS, axis=2)).astype(F32)
    weights = charges * live_mask
    stacked = jnp.concatenate([positions, weights[None]], axis=0)
    column_halo = padded(stacked, (("gz", 3),), SLOTS)
    extended = padded(column_halo, (("gx", 1), ("gy", 2)), 1)
    order = jnp.asarray(permutation(*sizes))
    vmem = pl.BlockSpec(memory_space=pltpu.VMEM)
    smem = pl.BlockSpec(memory_space=pltpu.SMEM)
    leaf, mid, upper = pl.pallas_call(
        lambda *refs: moment_kernel(block_z, *refs),
        out_shape=(
            jax.ShapeDtypeStruct((leaves, LANES), F32),
            jax.ShapeDtypeStruct((leaves // 8, LANES), F32),
            jax.ShapeDtypeStruct((8, LANES), F32),
        ),
        in_specs=[vmem] * 3,
        out_specs=(vmem, vmem, vmem),
        scratch_shapes=[pltpu.VMEM(((padded_terms + 1) * columns, column), F32)],
        name="moments",
    )(stacked.reshape(4, columns, column), moment_shift, order)
    axes = (("gx", 0), ("gy", 1), ("gz", 2))
    wide_leaf = padded(leaf.reshape(block_x, block_y, block_z, LANES), axes, 2)
    wide_mid = padded(mid.reshape(block_x // 2, block_y // 2, block_z // 2, LANES), axes, 2)
    wide_mid = jnp.pad(wide_mid, ((0, 0), (0, 0), (0, 8 - wide_mid.shape[2]), (0, 0)))
    uppers = lax.all_gather(upper[:1], ("gx", "gy", "gz"), axis=0, tiled=True)
    tops = moments_merge(
        uppers[:, :terms].reshape(number_x, number_y, number_z, terms), moment_shift.astype(F32)
    )
    root = jnp.sum(tops, axis=0, keepdims=True)
    top_count = tops.shape[0]
    top_sizes = (number_x // 2, number_y // 2, number_z // 2)
    shifts = offset_table()
    offsets = shifts.shape[0]
    upper_rows = (1 + top_count + 7) // 8 * 8
    at = (index_x, index_y, index_z)
    numbers = (number_x, number_y, number_z)
    picked = 0
    admitted = True
    for axis in range(3):
        picked = picked * numbers[axis] + (at[axis] + shifts[:, axis]) % numbers[axis]
        odd = at[axis] % 2
        admitted = admitted & (shifts[:, axis] >= -2 - odd) & (shifts[:, axis] <= 3 - odd)
    picked = jnp.where(admitted, picked, -1)
    entries = number_x * number_y * number_z
    static = np.full((offsets, upper_rows), -1, np.int32)
    for row in range(offsets):
        for box in range(top_count):
            spot = (
                box // (top_sizes[1] * top_sizes[2]),
                box // top_sizes[2] % top_sizes[1],
                box % top_sizes[2],
            )
            moved = [(spot[axis] + int(shifts[row, axis])) % top_sizes[axis] for axis in range(3)]
            static[row, 1 + box] = (
                entries + (moved[0] * top_sizes[1] + moved[1]) * top_sizes[2] + moved[2]
            )
    index = jnp.where(jnp.arange(upper_rows)[None, :] == 0, picked[:, None], jnp.asarray(static))
    table = jnp.concatenate([uppers[:, :terms], tops], axis=0)
    table = jnp.pad(table, ((0, 0), (0, LANES - terms)))
    rounded = lax.reduce_precision(table, 8, 7)
    both = jnp.concatenate([rounded, lax.reduce_precision(table - rounded, 8, 7)], axis=1)
    chosen = (index[:, :, None] == jnp.arange(entries + top_count)[None, None, :]).astype(BF16)
    upper_table = jnp.dot(
        chosen.reshape(offsets * upper_rows, -1), both.astype(BF16), preferred_element_type=F32
    ).reshape(offsets, upper_rows, 2 * LANES)
    parent = (index_x // 2 * top_sizes[1] + index_y // 2) * top_sizes[2] + index_z // 2
    octant = index_x % 2 * 4 + index_y % 2 * 2 + index_z % 2
    where = jnp.stack([parent, octant]).astype(jnp.int32)
    wide_x, wide_y = block_x + 5, block_y + 5
    half_x, half_y = block_x // 2, block_y // 2
    potential, field_out = pl.pallas_call(
        lambda *refs: field_kernel(sizes, top_count, *refs),
        out_shape=(
            jax.ShapeDtypeStruct((columns, column), F32),
            jax.ShapeDtypeStruct((3, columns, column), F32),
        ),
        in_specs=[smem, smem] + [vmem] * 10,
        out_specs=(vmem, vmem),
        scratch_shapes=[
            pltpu.VMEM((36, (block_x + 4) * block_y, column), F32),
            pltpu.VMEM((7, block_x + 4 + block_x, block_y + 4 + block_y, 8, LANES), F32),
            pltpu.VMEM((7, half_x + 4 + half_x, half_y + 4 + half_y, 8, LANES), F32),
            pltpu.VMEM((offsets // 2, padded_terms, 2 * LANES), BF16),
            pltpu.VMEM((upper_rows, terms), F32),
            pltpu.VMEM(((padded_terms + 1) * columns, column), F32),
            pltpu.VMEM((columns * 8 + half_x * half_y * 8 + 2 * upper_rows, padded_terms), F32),
        ],
        compiler_params=pltpu.CompilerParams(vmem_limit_bytes=60 * 1024 * 1024),
        name="fields",
    )(
        jnp.asarray(plan_table(block_x, block_y)),
        where,
        extended,
        live_mask.reshape(columns, column),
        wide_leaf,
        wide_mid,
        upper_table,
        root,
        far_operators,
        local_shift,
        lattice_operator,
        order,
    )
    return (
        potential.reshape(block_x, block_y, column),
        field_out.reshape(3, block_x, block_y, column),
    )


def solution(mesh):
    placed = (
        P(None, "gx", "gy", "gz"),
        P("gx", "gy", "gz"),
        P("gx", "gy", "gz"),
        P(),
        P(),
        P(),
        P(),
    )
    return jax.shard_map(
        per_device,
        mesh=mesh,
        in_specs=placed,
        out_specs=(P("gx", "gy", "gz"), P(None, "gx", "gy", "gz")),
        check_vma=False,
    )
```

```python
import jax
import jax.numpy as jnp
import numpy as np
from jax import lax
from jax.experimental import pallas as pl
from jax.experimental.pallas import tpu as pltpu
from jax.sharding import PartitionSpec as P

ORDER = 8
SLOTS = 32


SOFTENING = 0.0625


def padded(cells, sides, width):
    for axis, dim in sides:
        count = lax.axis_size(axis)
        head = lax.slice_in_dim(cells, 0, width, axis=dim)
        tail = lax.slice_in_dim(cells, cells.shape[dim] - width, cells.shape[dim], axis=dim)
        cells = jnp.concatenate(
            [
                lax.ppermute(tail, axis, [(i, (i + 1) % count) for i in range(count)]),
                cells,
                lax.ppermute(head, axis, [((i + 1) % count, i) for i in range(count)]),
            ],
            axis=dim,
        )
    return cells


def offset_table():
    listed = []
    for shift_x in range(-3, 4):
        for shift_y in range(-3, 4):
            for shift_z in range(-3, 4):
                if max(abs(shift_x), abs(shift_y), abs(shift_z)) >= 2:
                    listed.append((shift_x, shift_y, shift_z))
    return np.array(listed, dtype=np.int32)


def exponent_table(degree):
    listed = []
    for accumulated in range(degree + 1):
        for height in (0, 1):
            for power_x in range(accumulated - height + 1):
                listed.append((power_x, accumulated - height - power_x, height))
    return np.array(listed, dtype=np.int32)


NT = (((1,), (1,)), ((), ()))
TN = (((0,), (0,)), ((), ()))
F32 = jnp.float32
BF16 = jnp.bfloat16
LANES = 128


def split_rows(data):
    upper = data.astype(BF16)
    lower = (data - upper.astype(F32)).astype(BF16)
    return upper, lower


def apply(data, operator):
    upper, lower = split_rows(data)
    return lax.dot_general(upper, operator, NT, preferred_element_type=F32) + lax.dot_general(
        lower, operator, NT, preferred_element_type=F32
    )


def exact(left, right, dims):
    return lax.dot_general(
        left, right, dims, precision=lax.Precision.HIGHEST, preferred_element_type=F32
    )


def permutation(block_x, block_y, block_z):
    half_x, half_y, half_z = (block_x // 2, block_y // 2, block_z // 2)
    number = block_x * block_y * block_z
    table = np.zeros((number, number), np.float32)
    for x in range(block_x):
        for y in range(block_y):
            for z in range(block_z):
                octant = 4 * (x % 2) + 2 * (y % 2) + z % 2
                parent = (x // 2 * half_y + y // 2) * half_z + z // 2
                table[octant * (number // 8) + parent, (x * block_y + y) * block_z + z] = 1.0
    return table


def powers_of(values):
    listed = [jnp.ones_like(values)]
    for exponent in range(ORDER):
        listed.append(listed[-1] * values)
    return listed


def monomial_map(powers_x, powers_y, centred_z):
    made = {}
    for power_x, power_y, power_z in exponent_table(ORDER):
        key = (int(power_x), int(power_y), int(power_z))
        if key[2] == 0:
            made[key] = powers_x[key[0]] * powers_y[key[1]]
        else:
            made[key] = made[(key[0], key[1], 0)] * centred_z
    return made


def cell_picker(rows, cells):
    row = lax.broadcasted_iota(jnp.int32, (rows, cells * SLOTS), 0)
    lane = lax.broadcasted_iota(jnp.int32, (rows, cells * SLOTS), 1)
    return (lane // SLOTS == row).astype(F32)


def halo_slices(move, block, halo):
    if move == 1:
        return pl.ds(block, halo), pl.ds(0, halo)
    if move == -1:
        return pl.ds(halo, halo), pl.ds(block + halo, halo)
    return pl.ds(halo, block), pl.ds(halo, block)


def halo_copies(window, block, halo, numbers, at, sends, receives):
    copies = []
    for count in range(27):
        moves = (count // 9 - 1, count // 3 % 3 - 1, count % 3 - 1)
        if moves == (0, 0, 0):
            continue
        target = tuple(
            lax.rem(at[axis] + moves[axis] + numbers[axis], numbers[axis]) for axis in range(3)
        )
        from_x, to_x = halo_slices(moves[0], block[0], halo)
        from_y, to_y = halo_slices(moves[1], block[1], halo)
        copies.append(
            pltpu.make_async_remote_copy(
                src_ref=window.at[1, from_x, from_y],
                dst_ref=window.at[1 - moves[2], to_x, to_y],
                send_sem=sends.at[count],
                recv_sem=receives.at[count],
                device_id=target,
                device_id_type=pl.DeviceIdType.MESH,
            )
        )
    return copies


def local_moments(sizes, data_ref, shift_ref, order_ref, table, leaf_flat, leaf_wide, mid_wide, own_upper):
    block_x, block_y, cells = sizes
    terms = shift_ref.shape[1]
    columns = data_ref.shape[1]
    padded_terms = table.shape[0] // columns - 1
    powers_x = powers_of(data_ref[0] - 0.5)
    powers_x = [value * data_ref[3] for value in powers_x]
    powers_y = powers_of(data_ref[1] - 0.5)
    made = monomial_map(powers_x, powers_y, data_ref[2] - 0.5)
    for row, key in enumerate(exponent_table(ORDER)):
        table[row * columns : (row + 1) * columns, :] = made[tuple(int(v) for v in key)]
    spare = (padded_terms + 1 - terms) * columns
    table[terms * columns :, :] = jnp.zeros((spare, table.shape[1]), F32)
    picker = cell_picker(8, cells)
    for column in range(columns):
        rows = table[pl.ds(column, padded_terms, stride=columns), :]
        found = exact(picker, rows, NT)[:cells]
        found = jnp.concatenate([found, jnp.zeros((cells, LANES - padded_terms), F32)], axis=1)
        leaf_flat[column * cells : (column + 1) * cells, :] = found
        leaf_wide[1, 2 + column // block_y, 2 + column % block_y] = found
    ordered = exact(order_ref[...], leaf_flat[...], (((1,), (0,)), ((), ())))
    parents = ordered.shape[0] // 8
    mid = jnp.zeros((parents, terms), F32)
    for octant in range(8):
        piece = ordered[octant * parents : (octant + 1) * parents, :terms]
        mid = mid + apply(piece, shift_ref[octant])
    spare_lanes = jnp.zeros((8, LANES - terms), F32)
    mids = jnp.concatenate([mid, spare_lanes], axis=1)
    half_y, half_z = block_y // 2, cells // 2
    for column in range(block_x // 2 * half_y):
        mid_wide[1, 2 + column // half_y, 2 + column % half_y] = mids[
            column * half_z : (column + 1) * half_z
        ]
    up = jnp.zeros((8, terms), F32)
    for octant in range(8):
        piece = jnp.broadcast_to(mid[octant : octant + 1], (8, terms))
        up = up + apply(piece, shift_ref[octant])
    own_upper[...] = jnp.concatenate([up, spare_lanes], axis=1)


def field_kernel(
    sizes,
    numbers,
    plan_ref,
    where_ref,
    own_ref,
    data_ref,
    live_ref,
    shift_ref,
    far_ref,
    down_ref,
    lattice_ref,
    order_ref,
    merge_ref,
    chosen_ref,
    potential_ref,
    field_ref,
    near_wide,
    leaf_wide,
    mid_wide,
    uppers,
    leaf_flat,
    upper_rows_ref,
    spread,
    leaf_rows,
    mid_rows,
    operators,
    top_local,
    local_table,
    sums,
    sends,
    receives,
    upper_send,
    upper_receive,
):
    block_x, block_y, block_z = sizes
    columns = block_x * block_y
    width = block_z * SLOTS
    terms = down_ref.shape[1]
    offsets = plan_ref.shape[0] // 16
    padded_terms = operators.shape[1]

    at = tuple(lax.axis_index(axis) for axis in ("gx", "gy", "gz"))
    devices = numbers[0] * numbers[1] * numbers[2]
    rank = (at[0] * numbers[1] + at[1]) * numbers[2] + at[2]

    def coordinates(step):
        other = lax.rem(rank + step, devices)
        return (
            other // (numbers[1] * numbers[2]),
            lax.rem(other // numbers[2], numbers[1]),
            lax.rem(other, numbers[2]),
        )

    barrier = pltpu.get_barrier_semaphore()

    def greet(step, carry):
        pl.semaphore_signal(
            barrier, inc=1, device_id=coordinates(step), device_id_type=pl.DeviceIdType.MESH
        )
        return carry

    lax.fori_loop(1, devices, greet, 0)
    near_wide[1, 1 : 1 + block_x, 1 : 1 + block_y] = own_ref[...]
    own_slot = uppers.at[pl.ds(pl.multiple_of(rank * 8, 8), 8)]
    local_moments(
        sizes, data_ref, shift_ref, order_ref, local_table, leaf_flat, leaf_wide, mid_wide, own_slot
    )
    halves = (block_x // 2, block_y // 2)
    near_copies = halo_copies(near_wide, sizes, 1, numbers, at, sends.at[0], receives.at[0])
    leaf_copies = halo_copies(leaf_wide, sizes, 2, numbers, at, sends.at[1], receives.at[1])
    mid_copies = halo_copies(mid_wide, halves, 2, numbers, at, sends.at[2], receives.at[2])

    def upper_copy(step):
        return pltpu.make_async_remote_copy(
            src_ref=own_slot,
            dst_ref=own_slot,
            send_sem=upper_send.at[step],
            recv_sem=upper_receive.at[step],
            device_id=coordinates(step),
            device_id_type=pl.DeviceIdType.MESH,
        )

    def send_upper(step, carry):
        upper_copy(step).start()
        return carry

    def wait_upper(step, carry):
        upper_copy(step).wait()
        return carry

    pl.semaphore_wait(barrier, devices - 1)
    for copy in near_copies + leaf_copies + mid_copies:
        copy.start()
    lax.fori_loop(1, devices, send_upper, 0)

    def place(row, carry):
        start = row * terms
        base = jnp.minimum(start // LANES * LANES, far_ref.shape[1] - 2 * LANES)
        base = pl.multiple_of(base, LANES)
        held = far_ref[:, pl.ds(base, 2 * LANES)].astype(F32)
        held = jnp.concatenate(
            [held, jnp.zeros((padded_terms - terms, 2 * LANES), F32)], axis=0
        )
        turned = pltpu.roll(held, lax.rem(2 * LANES - (start - base), 2 * LANES), 1)
        return turned[:, :LANES].astype(BF16)

    def place_pair(pair, carry):
        operators[pair, :, :LANES] = place(2 * pair, carry)
        operators[pair, :, LANES:] = place(2 * pair + 1, carry)
        return carry

    lax.fori_loop(0, offsets // 2, place_pair, 0, unroll=2)

    lane = lax.broadcasted_iota(jnp.int32, (columns, width), 1)
    group = lane - lane % SLOTS
    turns = [group + (lane + step) % SLOTS for step in range(1, 5)]
    target_x = data_ref[0]
    target_y = data_ref[1]
    target_z = data_ref[2]
    for copy in near_copies:
        copy.wait()

    def fill(x, carry):
        for y in range(block_y + 2):
            low, own, high = (near_wide[0, x, y], near_wide[1, x, y], near_wide[2, x, y])
            moved = (
                jnp.concatenate([low[:, width - SLOTS :], own[:, : width - SLOTS]], axis=1),
                own,
                jnp.concatenate([own[:, SLOTS:], high[:, :SLOTS]], axis=1),
            )
            for move_y in range(3):
                if not 0 <= y - move_y < block_y:
                    continue
                for move_z in range(3):
                    for component in range(4):
                        spread[
                            (component * 3 + move_z) * 3 + move_y,
                            pl.ds(x * block_y + y - move_y, 1),
                            :,
                        ] = moved[move_z][component : component + 1]
        return carry

    lax.fori_loop(0, block_x + 2, fill, 0)

    def neighbour(which, totals):
        move_x = which // 9
        move_yz = which % 9
        move_y = move_yz // 3
        move_z = move_yz % 3
        slab = move_z * 3 + move_y
        rows = pl.ds(move_x * block_y, columns)
        shift_x = (move_x - 1).astype(F32)
        shift_y = (move_y - 1).astype(F32)
        shift_z = (move_z - 1).astype(F32)
        source = (
            spread[slab, rows, :] + shift_x,
            spread[9 + slab, rows, :] + shift_y,
            spread[18 + slab, rows, :] + shift_z,
            spread[27 + slab, rows, :],
        )
        own = which == 13

        def step(at, carry):
            held, totals = carry
            keep = jnp.where(own & (at == 0), 0.0, 1.0)
            sum_p, sum_x, sum_y, sum_z = totals
            for turn in range(4):
                if turn == 0:
                    s_x, s_y, s_z, s_q = held
                    s_q = s_q * keep
                else:
                    s_x, s_y, s_z, s_q = [
                        jnp.take_along_axis(value, turns[turn - 1], axis=1) for value in held
                    ]
                d_x = target_x - s_x
                d_y = target_y - s_y
                d_z = target_z - s_z
                inverse = lax.rsqrt(d_x * d_x + d_y * d_y + d_z * d_z + SOFTENING)
                weight = s_q * inverse
                sum_p = sum_p + weight
                cubic = weight * (inverse * inverse)
                sum_x = sum_x + cubic * d_x
                sum_y = sum_y + cubic * d_y
                sum_z = sum_z + cubic * d_z
            held = tuple(jnp.take_along_axis(value, turns[3], axis=1) for value in held)
            return held, (sum_p, sum_x, sum_y, sum_z)

        return lax.fori_loop(0, SLOTS // 4, step, (source, totals))[1]

    zero = jnp.zeros((columns, width), F32)
    near = lax.fori_loop(0, 27, neighbour, (zero, zero, zero, zero))

    row_of = lax.broadcasted_iota(jnp.int32, (8, LANES), 0)

    def sheets(held, cells, move):
        turned = pltpu.roll(held, (8 - (move + 2)) % 8, 0)
        if move == 3:
            turned = jnp.where(row_of % 2 == 0, turned, 0.0)
        if move == -3:
            turned = jnp.where(row_of % 2 == 1, turned, 0.0)
        upper = turned.astype(BF16).astype(F32)
        lower = pltpu.roll(turned - upper, cells, 0)
        made = jnp.where(row_of < cells, upper, lower)
        return jnp.where(row_of < 2 * cells, made, 0.0)

    for copy in leaf_copies + mid_copies:
        copy.wait()
    lax.fori_loop(1, devices, wait_upper, 0)
    wide_x, wide_y = leaf_wide.shape[1], leaf_wide.shape[2]
    leaf_rows[...] = jnp.zeros(leaf_rows.shape, F32)
    mid_rows[...] = jnp.zeros(mid_rows.shape, F32)

    def leaf_sheet(at, carry):
        x = at // wide_y
        y = at % wide_y
        held = jnp.concatenate(
            [leaf_wide[0, x, y][block_z - 2 :], leaf_wide[1, x, y], leaf_wide[2, x, y][:2]], axis=0
        )
        for move in range(-3, 4):
            leaf_rows[move + 3, x, y] = sheets(held, block_z, move)
        return carry

    lax.fori_loop(0, wide_x * wide_y, leaf_sheet, 0)
    mid_x, mid_y = mid_wide.shape[1], mid_wide.shape[2]

    def mid_sheet(at, carry):
        x = at // mid_y
        y = at % mid_y
        held = jnp.concatenate(
            [mid_wide[0, x, y], mid_wide[1, x, y], mid_wide[2, x, y], jnp.zeros((2, LANES), F32)],
            axis=0,
        )
        for move in range(-3, 4):
            mid_rows[move + 3, x, y] = sheets(held, block_z // 2, move)
        return carry

    lax.fori_loop(0, mid_x * mid_y, mid_sheet, 0)

    half_x, half_y = block_x // 2, block_y // 2
    upper_rows = chosen_ref.shape[1]
    all_upper = uppers[pl.ds(0, devices, stride=8), :]
    sorted_upper = exact(merge_ref[...], all_upper, (((1,), (0,)), ((), ())))
    tops = devices // 8
    merged = jnp.zeros((tops, terms), F32)
    for octant in range(8):
        merged = merged + apply(sorted_upper[octant * tops : (octant + 1) * tops, :terms], shift_ref[octant])
    root = jnp.sum(merged, axis=0, keepdims=True)
    merged = jnp.concatenate([merged, jnp.zeros((tops, LANES - terms), F32)], axis=1)
    both = jnp.concatenate(split_rows(jnp.concatenate([all_upper, merged], axis=0)), axis=1)

    def pick(group, carry):
        found = jnp.dot(
            chosen_ref[pl.ds(group * 4, 4)].reshape(4 * upper_rows, -1).astype(BF16),
            both,
            preferred_element_type=F32,
        )
        upper_rows_ref[pl.ds(group * 4, 4)] = found.reshape(4, upper_rows, 2 * LANES)
        return carry

    lax.fori_loop(0, offsets // 4, pick, 0)

    def gathered(row):
        at = row * 16
        move_z = plan_ref[at + 2]
        pieces = []
        for x in range(block_x):
            for y in range(block_y):
                pieces.append(leaf_rows[move_z, plan_ref[at + 4 + x % 2] + x, plan_ref[at + 6 + y % 2] + y])
        for x in range(half_x):
            for y in range(half_y):
                pieces.append(mid_rows[move_z, plan_ref[at + 8 + x % 2] + x, plan_ref[at + 10 + y % 2] + y])
        pieces.append(upper_rows_ref[row, :, :LANES])
        pieces.append(upper_rows_ref[row, :, LANES:])
        return jnp.concatenate(pieces, axis=0).astype(BF16)

    def far_step(pair, total):
        left = jnp.concatenate([gathered(2 * pair), gathered(2 * pair + 1)], axis=1)
        return total + lax.dot_general(left, operators[pair], NT, preferred_element_type=F32)

    leaf_count = columns * 8
    mid_count = half_x * half_y * 8
    total_rows = leaf_count + mid_count + 2 * upper_rows
    sums[...] = lax.fori_loop(
        0, offsets // 2, far_step, jnp.zeros((total_rows, padded_terms), F32), unroll=2
    )
    first = leaf_count + mid_count
    far_high = sums[first : first + upper_rows, :terms] + sums[first + upper_rows :, :terms]
    lattice = apply(jnp.broadcast_to(root, (8, terms)), lattice_ref[...])
    top_local[...] = 0.125 * (far_high + lattice[:1])
    parent = top_local[pl.ds(where_ref[0] + 1, 1), :]
    upper = 0.25 * far_high[:1] + apply(jnp.broadcast_to(parent, (8, terms)), down_ref[where_ref[1]])[:1]
    upper = jnp.broadcast_to(upper, (8, terms))
    half_z = block_z // 2
    mids = jnp.concatenate([apply(upper, down_ref[octant])[:1] for octant in range(8)], axis=0)
    far_mids = []
    for column in range(half_x * half_y):
        held = sums[leaf_count + column * 8 : leaf_count + column * 8 + 8, :terms]
        far_mids.append(held[:half_z] + held[half_z : 2 * half_z])
    mids = mids + 0.5 * jnp.concatenate(far_mids, axis=0)
    pieces = [apply(mids, down_ref[octant]) for octant in range(8)]
    downs = exact(order_ref[...], jnp.concatenate(pieces, axis=0), TN)
    picker = cell_picker(block_z, block_z)
    for column in range(columns):
        held = sums[column * 8 : column * 8 + 8, :terms]
        local = held[:block_z] + held[block_z : 2 * block_z]
        local = local + downs[column * block_z : (column + 1) * block_z]
        local_table[pl.ds(column, terms, stride=columns), :] = exact(local, picker, TN)

    made = monomial_map(powers_of(target_x - 0.5), powers_of(target_y - 0.5), target_z - 0.5)
    out_p, out_x, out_y, out_z = near
    for row, key in enumerate(exponent_table(ORDER)):
        power_x, power_y, power_z = [int(v) for v in key]
        local = local_table[row * columns : (row + 1) * columns, :]
        out_p = out_p + local * made[(power_x, power_y, power_z)]
        if power_x:
            out_x = out_x - (float(power_x) * local) * made[(power_x - 1, power_y, power_z)]
        if power_y:
            out_y = out_y - (float(power_y) * local) * made[(power_x, power_y - 1, power_z)]
        if power_z:
            out_z = out_z - local * made[(power_x, power_y, 0)]
    live = live_ref[...]
    potential_ref[...] = out_p * live
    field_ref[0] = out_x * live
    field_ref[1] = out_y * live
    field_ref[2] = out_z * live


def plan_table(block_x, block_y):
    shifts = offset_table()
    plan = np.zeros((shifts.shape[0], 16), np.int32)
    for row, shift in enumerate(shifts):
        for axis in range(3):
            plan[row, axis] = shift[axis] + 3
        for axis in range(2):
            block = (block_x, block_y)[axis]
            for odd in range(2):
                admitted = -2 - odd <= shift[axis] <= 3 - odd
                plan[row, 4 + 2 * axis + odd] = shift[axis] + 2 if admitted else block + 4
                plan[row, 8 + 2 * axis + odd] = shift[axis] + 2 if admitted else block // 2 + 4
    return plan.reshape(-1)


def per_device(
    positions, charges, counts, moment_shift, far_operators, local_shift, lattice_operator
):
    block_x, block_y, column = charges.shape
    block_z = column // SLOTS
    sizes = (block_x, block_y, block_z)
    number_x = lax.axis_size("gx")
    number_y = lax.axis_size("gy")
    number_z = lax.axis_size("gz")
    index_x = lax.axis_index("gx")
    index_y = lax.axis_index("gy")
    index_z = lax.axis_index("gz")
    terms = moment_shift.shape[1]
    padded_terms = (terms + 15) // 16 * 16
    columns = block_x * block_y
    leaves = columns * block_z
    slot_of = jnp.arange(column, dtype=jnp.int32) % SLOTS
    live_mask = (slot_of[None, None, :] < jnp.repeat(counts, SLOTS, axis=2)).astype(F32)
    weights = charges * live_mask
    stacked = jnp.concatenate([positions, weights[None]], axis=0)
    order = jnp.asarray(permutation(*sizes))
    vmem = pl.BlockSpec(memory_space=pltpu.VMEM)
    smem = pl.BlockSpec(memory_space=pltpu.SMEM)
    top_count = number_x * number_y * number_z // 8
    top_sizes = (number_x // 2, number_y // 2, number_z // 2)
    shifts = offset_table()
    offsets = shifts.shape[0]
    upper_rows = (1 + top_count + 7) // 8 * 8
    at = (index_x, index_y, index_z)
    numbers = (number_x, number_y, number_z)
    picked = 0
    admitted = True
    for axis in range(3):
        picked = picked * numbers[axis] + (at[axis] + shifts[:, axis]) % numbers[axis]
        odd = at[axis] % 2
        admitted = admitted & (shifts[:, axis] >= -2 - odd) & (shifts[:, axis] <= 3 - odd)
    picked = jnp.where(admitted, picked, -1)
    entries = number_x * number_y * number_z
    static = np.full((offsets, upper_rows), -1, np.int32)
    for row in range(offsets):
        for box in range(top_count):
            spot = (
                box // (top_sizes[1] * top_sizes[2]),
                box // top_sizes[2] % top_sizes[1],
                box % top_sizes[2],
            )
            moved = [(spot[axis] + int(shifts[row, axis])) % top_sizes[axis] for axis in range(3)]
            static[row, 1 + box] = (
                entries + (moved[0] * top_sizes[1] + moved[1]) * top_sizes[2] + moved[2]
            )
    index = jnp.where(jnp.arange(upper_rows)[None, :] == 0, picked[:, None], jnp.asarray(static))
    chosen = (index[:, :, None] == jnp.arange(entries + top_count)[None, None, :]).astype(F32)
    parent = (index_x // 2 * top_sizes[1] + index_y // 2) * top_sizes[2] + index_z // 2
    octant = index_x % 2 * 4 + index_y % 2 * 2 + index_z % 2
    where = jnp.stack([parent, octant]).astype(jnp.int32)
    wide_x, wide_y = block_x + 5, block_y + 5
    half_x, half_y = block_x // 2, block_y // 2
    potential, field_out = pl.pallas_call(
        lambda *refs: field_kernel(sizes, numbers, *refs),
        out_shape=(
            jax.ShapeDtypeStruct((columns, column), F32),
            jax.ShapeDtypeStruct((3, columns, column), F32),
        ),
        in_specs=[smem, smem] + [vmem] * 10,
        out_specs=(vmem, vmem),
        scratch_shapes=[
            pltpu.VMEM((3, block_x + 2, block_y + 2, 4, column), F32),
            pltpu.VMEM((3, block_x + 4, block_y + 4, block_z, LANES), F32),
            pltpu.VMEM((3, half_x + 4, half_y + 4, block_z // 2, LANES), F32),
            pltpu.VMEM((entries * 8 + 8, LANES), F32),
            pltpu.VMEM((leaves, LANES), F32),
            pltpu.VMEM((offsets, upper_rows, 2 * LANES), F32),
            pltpu.VMEM((36, (block_x + 4) * block_y, column), F32),
            pltpu.VMEM((7, block_x + 4 + block_x, block_y + 4 + block_y, 8, LANES), F32),
            pltpu.VMEM((7, half_x + 4 + half_x, half_y + 4 + half_y, 8, LANES), F32),
            pltpu.VMEM((offsets // 2, padded_terms, 2 * LANES), BF16),
            pltpu.VMEM((upper_rows, terms), F32),
            pltpu.VMEM(((padded_terms + 1) * columns, column), F32),
            pltpu.VMEM((columns * 8 + half_x * half_y * 8 + 2 * upper_rows, padded_terms), F32),
            pltpu.SemaphoreType.DMA((3, 27)),
            pltpu.SemaphoreType.DMA((3, 27)),
            pltpu.SemaphoreType.DMA((entries,)),
            pltpu.SemaphoreType.DMA((entries,)),
        ],
        compiler_params=pltpu.CompilerParams(
            vmem_limit_bytes=60 * 1024 * 1024, collective_id=0, has_side_effects=True
        ),
        name="fields",
    )(
        jnp.asarray(plan_table(block_x, block_y)),
        where,
        jnp.transpose(stacked, (1, 2, 0, 3)),
        stacked.reshape(4, columns, column),
        live_mask.reshape(columns, column),
        moment_shift,
        far_operators,
        local_shift,
        lattice_operator,
        order,
        jnp.asarray(permutation(*numbers)),
        chosen,
    )
    return (
        potential.reshape(block_x, block_y, column),
        field_out.reshape(3, block_x, block_y, column),
    )


def solution(mesh):
    placed = (
        P(None, "gx", "gy", "gz"),
        P("gx", "gy", "gz"),
        P("gx", "gy", "gz"),
        P(),
        P(),
        P(),
        P(),
    )
    return jax.shard_map(
        per_device,
        mesh=mesh,
        in_specs=placed,
        out_specs=(P("gx", "gy", "gz"), P(None, "gx", "gy", "gz")),
        check_vma=False,
    )
```

```python
import jax
import jax.numpy as jnp
import numpy as np
from jax import lax
from jax.experimental import pallas as pl
from jax.experimental.pallas import tpu as pltpu
from jax.sharding import PartitionSpec as P

ORDER = 8
SLOTS = 32


SOFTENING = 0.0625


def padded(cells, sides, width):
    for axis, dim in sides:
        count = lax.axis_size(axis)
        head = lax.slice_in_dim(cells, 0, width, axis=dim)
        tail = lax.slice_in_dim(cells, cells.shape[dim] - width, cells.shape[dim], axis=dim)
        cells = jnp.concatenate(
            [
                lax.ppermute(tail, axis, [(i, (i + 1) % count) for i in range(count)]),
                cells,
                lax.ppermute(head, axis, [((i + 1) % count, i) for i in range(count)]),
            ],
            axis=dim,
        )
    return cells


def offset_table():
    listed = []
    for shift_x in range(-3, 4):
        for shift_y in range(-3, 4):
            for shift_z in range(-3, 4):
                if max(abs(shift_x), abs(shift_y), abs(shift_z)) >= 2:
                    listed.append((shift_x, shift_y, shift_z))
    return np.array(listed, dtype=np.int32)


def exponent_table(degree):
    listed = []
    for accumulated in range(degree + 1):
        for height in (0, 1):
            for power_x in range(accumulated - height + 1):
                listed.append((power_x, accumulated - height - power_x, height))
    return np.array(listed, dtype=np.int32)


NT = (((1,), (1,)), ((), ()))
TN = (((0,), (0,)), ((), ()))
F32 = jnp.float32
BF16 = jnp.bfloat16
LANES = 128


def split_rows(data):
    upper = data.astype(BF16)
    lower = (data - upper.astype(F32)).astype(BF16)
    return upper, lower


def apply(data, operator):
    upper, lower = split_rows(data)
    return lax.dot_general(upper, operator, NT, preferred_element_type=F32) + lax.dot_general(
        lower, operator, NT, preferred_element_type=F32
    )


def exact(left, right, dims):
    return lax.dot_general(
        left, right, dims, precision=lax.Precision.HIGHEST, preferred_element_type=F32
    )


def permutation(block_x, block_y, block_z):
    half_x, half_y, half_z = (block_x // 2, block_y // 2, block_z // 2)
    number = block_x * block_y * block_z
    table = np.zeros((number, number), np.float32)
    for x in range(block_x):
        for y in range(block_y):
            for z in range(block_z):
                octant = 4 * (x % 2) + 2 * (y % 2) + z % 2
                parent = (x // 2 * half_y + y // 2) * half_z + z // 2
                table[octant * (number // 8) + parent, (x * block_y + y) * block_z + z] = 1.0
    return table


def powers_of(values):
    listed = [jnp.ones_like(values)]
    for exponent in range(ORDER):
        listed.append(listed[-1] * values)
    return listed


def monomial_map(powers_x, powers_y, centred_z):
    made = {}
    for power_x, power_y, power_z in exponent_table(ORDER):
        key = (int(power_x), int(power_y), int(power_z))
        if key[2] == 0:
            made[key] = powers_x[key[0]] * powers_y[key[1]]
        else:
            made[key] = made[(key[0], key[1], 0)] * centred_z
    return made


def cell_picker(rows, cells):
    row = lax.broadcasted_iota(jnp.int32, (rows, cells * SLOTS), 0)
    lane = lax.broadcasted_iota(jnp.int32, (rows, cells * SLOTS), 1)
    return (lane // SLOTS == row).astype(F32)


def halo_slices(move, block, halo):
    if move == 1:
        return pl.ds(block, halo), pl.ds(0, halo)
    if move == -1:
        return pl.ds(halo, halo), pl.ds(block + halo, halo)
    return pl.ds(halo, block), pl.ds(halo, block)


def halo_copies(window, block, halo, numbers, at, sends, receives):
    copies = []
    for count in range(27):
        moves = (count // 9 - 1, count // 3 % 3 - 1, count % 3 - 1)
        if moves == (0, 0, 0):
            continue
        target = tuple(
            lax.rem(at[axis] + moves[axis] + numbers[axis], numbers[axis]) for axis in range(3)
        )
        from_x, to_x = halo_slices(moves[0], block[0], halo)
        from_y, to_y = halo_slices(moves[1], block[1], halo)
        copies.append(
            pltpu.make_async_remote_copy(
                src_ref=window.at[1, from_x, from_y],
                dst_ref=window.at[1 - moves[2], to_x, to_y],
                send_sem=sends.at[count],
                recv_sem=receives.at[count],
                device_id=target,
                device_id_type=pl.DeviceIdType.MESH,
            )
        )
    return copies


def local_moments(sizes, data_ref, shift_ref, order_ref, table, leaf_flat, leaf_wide, mid_wide, own_upper):
    block_x, block_y, cells = sizes
    terms = shift_ref.shape[1]
    columns = data_ref.shape[1]
    padded_terms = table.shape[0] // columns - 1
    powers_x = powers_of(data_ref[0] - 0.5)
    powers_x = [value * data_ref[3] for value in powers_x]
    powers_y = powers_of(data_ref[1] - 0.5)
    made = monomial_map(powers_x, powers_y, data_ref[2] - 0.5)
    for row, key in enumerate(exponent_table(ORDER)):
        table[row * columns : (row + 1) * columns, :] = made[tuple(int(v) for v in key)]
    spare = (padded_terms + 1 - terms) * columns
    table[terms * columns :, :] = jnp.zeros((spare, table.shape[1]), F32)
    picker = cell_picker(8, cells)
    for column in range(columns):
        rows = table[pl.ds(column, padded_terms, stride=columns), :]
        found = exact(picker, rows, NT)[:cells]
        found = jnp.concatenate([found, jnp.zeros((cells, LANES - padded_terms), F32)], axis=1)
        leaf_flat[column * cells : (column + 1) * cells, :] = found
        leaf_wide[1, 2 + column // block_y, 2 + column % block_y] = found
    ordered = exact(order_ref[...], leaf_flat[...], (((1,), (0,)), ((), ())))
    parents = ordered.shape[0] // 8
    mid = jnp.zeros((parents, terms), F32)
    for octant in range(8):
        piece = ordered[octant * parents : (octant + 1) * parents, :terms]
        mid = mid + apply(piece, shift_ref[octant])
    spare_lanes = jnp.zeros((8, LANES - terms), F32)
    mids = jnp.concatenate([mid, spare_lanes], axis=1)
    half_y, half_z = block_y // 2, cells // 2
    for column in range(block_x // 2 * half_y):
        mid_wide[1, 2 + column // half_y, 2 + column % half_y] = mids[
            column * half_z : (column + 1) * half_z
        ]
    up = jnp.zeros((8, terms), F32)
    for octant in range(8):
        piece = jnp.broadcast_to(mid[octant : octant + 1], (8, terms))
        up = up + apply(piece, shift_ref[octant])
    own_upper[...] = jnp.concatenate([up, spare_lanes], axis=1)


def field_kernel(
    sizes,
    numbers,
    plan_ref,
    where_ref,
    own_ref,
    data_ref,
    live_ref,
    shift_ref,
    far_ref,
    down_ref,
    lattice_ref,
    order_ref,
    merge_ref,
    chosen_ref,
    potential_ref,
    field_ref,
    near_wide,
    leaf_wide,
    mid_wide,
    uppers,
    leaf_flat,
    upper_rows_ref,
    spread,
    leaf_rows,
    mid_rows,
    operators,
    top_local,
    local_table,
    sums,
    sends,
    receives,
    upper_send,
    upper_receive,
):
    block_x, block_y, block_z = sizes
    columns = block_x * block_y
    width = block_z * SLOTS
    terms = down_ref.shape[1]
    offsets = plan_ref.shape[0] // 16
    padded_terms = operators.shape[1]

    at = tuple(lax.axis_index(axis) for axis in ("gx", "gy", "gz"))
    devices = numbers[0] * numbers[1] * numbers[2]
    rank = (at[0] * numbers[1] + at[1]) * numbers[2] + at[2]

    def coordinates(step):
        other = lax.rem(rank + step, devices)
        return (
            other // (numbers[1] * numbers[2]),
            lax.rem(other // numbers[2], numbers[1]),
            lax.rem(other, numbers[2]),
        )

    barrier = pltpu.get_barrier_semaphore()

    def greet(step, carry):
        pl.semaphore_signal(
            barrier, inc=1, device_id=coordinates(step), device_id_type=pl.DeviceIdType.MESH
        )
        return carry

    lax.fori_loop(1, devices, greet, 0)
    near_wide[1, 1 : 1 + block_x, 1 : 1 + block_y] = own_ref[...]
    own_slot = uppers.at[pl.ds(pl.multiple_of(rank * 8, 8), 8)]
    local_moments(
        sizes, data_ref, shift_ref, order_ref, local_table, leaf_flat, leaf_wide, mid_wide, own_slot
    )
    halves = (block_x // 2, block_y // 2)
    near_copies = halo_copies(near_wide, sizes, 1, numbers, at, sends.at[0], receives.at[0])
    leaf_copies = halo_copies(leaf_wide, sizes, 2, numbers, at, sends.at[1], receives.at[1])
    mid_copies = halo_copies(mid_wide, halves, 2, numbers, at, sends.at[2], receives.at[2])

    def upper_copy(step):
        return pltpu.make_async_remote_copy(
            src_ref=own_slot,
            dst_ref=own_slot,
            send_sem=upper_send.at[step],
            recv_sem=upper_receive.at[step],
            device_id=coordinates(step),
            device_id_type=pl.DeviceIdType.MESH,
        )

    def send_upper(step, carry):
        upper_copy(step).start()
        return carry

    def wait_upper(step, carry):
        upper_copy(step).wait()
        return carry

    pl.semaphore_wait(barrier, devices - 1)
    for copy in near_copies + leaf_copies + mid_copies:
        copy.start()
    lax.fori_loop(1, devices, send_upper, 0)

    def place(row, carry):
        start = row * terms
        base = jnp.minimum(start & -LANES, far_ref.shape[1] - 2 * LANES)
        base = pl.multiple_of(base, LANES)
        held = far_ref[:, pl.ds(base, 2 * LANES)].astype(F32)
        held = jnp.concatenate(
            [held, jnp.zeros((padded_terms - terms, 2 * LANES), F32)], axis=0
        )
        turned = pltpu.roll(held, (2 * LANES - (start - base)) & (2 * LANES - 1), 1)
        return turned[:, :LANES].astype(BF16)

    def place_pair(pair, carry):
        for which in range(2):
            operators[2 * pair + which, :, :LANES] = place(4 * pair + 2 * which, carry)
            operators[2 * pair + which, :, LANES:] = place(4 * pair + 2 * which + 1, carry)
        return carry

    lax.fori_loop(0, offsets // 4, place_pair, 0)

    lane = lax.broadcasted_iota(jnp.int32, (columns, width), 1)
    group = lane - lane % SLOTS
    turns = [group + (lane + step) % SLOTS for step in range(1, 9)]
    target_x = data_ref[0]
    target_y = data_ref[1]
    target_z = data_ref[2]
    for copy in near_copies:
        copy.wait()

    def fill(x, carry):
        for y in range(block_y + 2):
            low, own, high = (near_wide[0, x, y], near_wide[1, x, y], near_wide[2, x, y])
            moved = (
                jnp.concatenate([low[:, width - SLOTS :], own[:, : width - SLOTS]], axis=1),
                own,
                jnp.concatenate([own[:, SLOTS:], high[:, :SLOTS]], axis=1),
            )
            for move_y in range(3):
                if not 0 <= y - move_y < block_y:
                    continue
                for move_z in range(3):
                    for component in range(4):
                        spread[
                            (component * 3 + move_z) * 3 + move_y,
                            pl.ds(x * block_y + y - move_y, 1),
                            :,
                        ] = moved[move_z][component : component + 1]
        return carry

    lax.fori_loop(0, block_x + 2, fill, 0)

    def neighbour(which, totals):
        move_x = which // 9
        move_yz = which % 9
        move_y = move_yz // 3
        move_z = move_yz % 3
        slab = move_z * 3 + move_y
        rows = pl.ds(move_x * block_y, columns)
        shift_x = (move_x - 1).astype(F32)
        shift_y = (move_y - 1).astype(F32)
        shift_z = (move_z - 1).astype(F32)
        source = (
            spread[slab, rows, :] + shift_x,
            spread[9 + slab, rows, :] + shift_y,
            spread[18 + slab, rows, :] + shift_z,
            spread[27 + slab, rows, :],
        )
        own = which == 13

        def step(at, carry):
            held, totals = carry
            keep = jnp.where(own & (at == 0), 0.0, 1.0)
            sum_p, sum_x, sum_y, sum_z = totals
            for turn in range(8):
                if turn == 0:
                    s_x, s_y, s_z, s_q = held
                    s_q = s_q * keep
                else:
                    s_x, s_y, s_z, s_q = [
                        jnp.take_along_axis(value, turns[turn - 1], axis=1) for value in held
                    ]
                d_x = target_x - s_x
                d_y = target_y - s_y
                d_z = target_z - s_z
                inverse = lax.rsqrt(d_x * d_x + d_y * d_y + d_z * d_z + SOFTENING)
                weight = s_q * inverse
                sum_p = sum_p + weight
                cubic = weight * (inverse * inverse)
                sum_x = sum_x + cubic * d_x
                sum_y = sum_y + cubic * d_y
                sum_z = sum_z + cubic * d_z
            held = tuple(jnp.take_along_axis(value, turns[7], axis=1) for value in held)
            return held, (sum_p, sum_x, sum_y, sum_z)

        return lax.fori_loop(0, SLOTS // 8, step, (source, totals))[1]

    zero = jnp.zeros((columns, width), F32)
    near = lax.fori_loop(0, 27, neighbour, (zero, zero, zero, zero))

    row_of = lax.broadcasted_iota(jnp.int32, (8, LANES), 0)

    def sheets(held, cells, move):
        turned = pltpu.roll(held, (8 - (move + 2)) % 8, 0)
        if move == 3:
            turned = jnp.where(row_of % 2 == 0, turned, 0.0)
        if move == -3:
            turned = jnp.where(row_of % 2 == 1, turned, 0.0)
        upper = turned.astype(BF16).astype(F32)
        lower = pltpu.roll(turned - upper, cells, 0)
        made = jnp.where(row_of < cells, upper, lower)
        return jnp.where(row_of < 2 * cells, made, 0.0)

    for copy in leaf_copies + mid_copies:
        copy.wait()
    lax.fori_loop(1, devices, wait_upper, 0)
    wide_x, wide_y = leaf_wide.shape[1], leaf_wide.shape[2]
    leaf_rows[...] = jnp.zeros(leaf_rows.shape, F32)
    mid_rows[...] = jnp.zeros(mid_rows.shape, F32)

    def leaf_sheet(at, carry):
        x = at // wide_y
        y = at % wide_y
        held = jnp.concatenate(
            [leaf_wide[0, x, y][block_z - 2 :], leaf_wide[1, x, y], leaf_wide[2, x, y][:2]], axis=0
        )
        for move in range(-3, 4):
            leaf_rows[move + 3, x, y] = sheets(held, block_z, move)
        return carry

    lax.fori_loop(0, wide_x * wide_y, leaf_sheet, 0)
    mid_x, mid_y = mid_wide.shape[1], mid_wide.shape[2]

    def mid_sheet(at, carry):
        x = at // mid_y
        y = at % mid_y
        held = jnp.concatenate(
            [mid_wide[0, x, y], mid_wide[1, x, y], mid_wide[2, x, y], jnp.zeros((2, LANES), F32)],
            axis=0,
        )
        for move in range(-3, 4):
            mid_rows[move + 3, x, y] = sheets(held, block_z // 2, move)
        return carry

    lax.fori_loop(0, mid_x * mid_y, mid_sheet, 0)

    half_x, half_y = block_x // 2, block_y // 2
    upper_rows = chosen_ref.shape[1]
    all_upper = uppers[pl.ds(0, devices, stride=8), :]
    sorted_upper = exact(merge_ref[...], all_upper, (((1,), (0,)), ((), ())))
    tops = devices // 8
    merged = jnp.zeros((tops, terms), F32)
    for octant in range(8):
        merged = merged + apply(sorted_upper[octant * tops : (octant + 1) * tops, :terms], shift_ref[octant])
    root = jnp.sum(merged, axis=0, keepdims=True)
    merged = jnp.concatenate([merged, jnp.zeros((tops, LANES - terms), F32)], axis=1)
    both = jnp.concatenate(split_rows(jnp.concatenate([all_upper, merged], axis=0)), axis=1)

    def pick(group, carry):
        found = jnp.dot(
            chosen_ref[pl.ds(group * 4, 4)].reshape(4 * upper_rows, -1).astype(BF16),
            both,
            preferred_element_type=F32,
        )
        upper_rows_ref[pl.ds(group * 4, 4)] = found.reshape(4, upper_rows, 2 * LANES)
        return carry

    lax.fori_loop(0, offsets // 4, pick, 0)

    def gathered(row):
        at = row * 16
        move_z = plan_ref[at + 2]
        pieces = []
        for x in range(block_x):
            for y in range(block_y):
                pieces.append(leaf_rows[move_z, plan_ref[at + 4 + x % 2] + x, plan_ref[at + 6 + y % 2] + y])
        for x in range(half_x):
            for y in range(half_y):
                pieces.append(mid_rows[move_z, plan_ref[at + 8 + x % 2] + x, plan_ref[at + 10 + y % 2] + y])
        pieces.append(upper_rows_ref[row, :, :LANES])
        pieces.append(upper_rows_ref[row, :, LANES:])
        return jnp.concatenate(pieces, axis=0).astype(BF16)

    def far_step(pair, total):
        added = []
        for which in range(2):
            row = 4 * pair + 2 * which
            left = jnp.concatenate([gathered(row), gathered(row + 1)], axis=1)
            added.append(
                lax.dot_general(left, operators[2 * pair + which], NT, preferred_element_type=F32)
            )
        return total + (added[0] + added[1])

    leaf_count = columns * 8
    mid_count = half_x * half_y * 8
    total_rows = leaf_count + mid_count + 2 * upper_rows
    sums[...] = lax.fori_loop(
        0, offsets // 4, far_step, jnp.zeros((total_rows, padded_terms), F32)
    )
    first = leaf_count + mid_count
    far_high = sums[first : first + upper_rows, :terms] + sums[first + upper_rows :, :terms]
    lattice = apply(jnp.broadcast_to(root, (8, terms)), lattice_ref[...])
    top_local[...] = 0.125 * (far_high + lattice[:1])
    parent = top_local[pl.ds(where_ref[0] + 1, 1), :]
    upper = 0.25 * far_high[:1] + apply(jnp.broadcast_to(parent, (8, terms)), down_ref[where_ref[1]])[:1]
    upper = jnp.broadcast_to(upper, (8, terms))
    half_z = block_z // 2
    mids = jnp.concatenate([apply(upper, down_ref[octant])[:1] for octant in range(8)], axis=0)
    far_mids = []
    for column in range(half_x * half_y):
        held = sums[leaf_count + column * 8 : leaf_count + column * 8 + 8, :terms]
        far_mids.append(held[:half_z] + held[half_z : 2 * half_z])
    mids = mids + 0.5 * jnp.concatenate(far_mids, axis=0)
    pieces = [apply(mids, down_ref[octant]) for octant in range(8)]
    downs = exact(order_ref[...], jnp.concatenate(pieces, axis=0), TN)
    picker = cell_picker(block_z, block_z)
    for column in range(columns):
        held = sums[column * 8 : column * 8 + 8, :terms]
        local = held[:block_z] + held[block_z : 2 * block_z]
        local = local + downs[column * block_z : (column + 1) * block_z]
        local_table[pl.ds(column, terms, stride=columns), :] = exact(local, picker, TN)

    made = monomial_map(powers_of(target_x - 0.5), powers_of(target_y - 0.5), target_z - 0.5)
    out_p, out_x, out_y, out_z = near
    for row, key in enumerate(exponent_table(ORDER)):
        power_x, power_y, power_z = [int(v) for v in key]
        local = local_table[row * columns : (row + 1) * columns, :]
        out_p = out_p + local * made[(power_x, power_y, power_z)]
        if power_x:
            out_x = out_x - (float(power_x) * local) * made[(power_x - 1, power_y, power_z)]
        if power_y:
            out_y = out_y - (float(power_y) * local) * made[(power_x, power_y - 1, power_z)]
        if power_z:
            out_z = out_z - local * made[(power_x, power_y, 0)]
    live = live_ref[...]
    potential_ref[...] = out_p * live
    field_ref[0] = out_x * live
    field_ref[1] = out_y * live
    field_ref[2] = out_z * live


def plan_table(block_x, block_y):
    shifts = offset_table()
    plan = np.zeros((shifts.shape[0], 16), np.int32)
    for row, shift in enumerate(shifts):
        for axis in range(3):
            plan[row, axis] = shift[axis] + 3
        for axis in range(2):
            block = (block_x, block_y)[axis]
            for odd in range(2):
                admitted = -2 - odd <= shift[axis] <= 3 - odd
                plan[row, 4 + 2 * axis + odd] = shift[axis] + 2 if admitted else block + 4
                plan[row, 8 + 2 * axis + odd] = shift[axis] + 2 if admitted else block // 2 + 4
    return plan.reshape(-1)


def per_device(
    positions, charges, counts, moment_shift, far_operators, local_shift, lattice_operator
):
    block_x, block_y, column = charges.shape
    block_z = column // SLOTS
    sizes = (block_x, block_y, block_z)
    number_x = lax.axis_size("gx")
    number_y = lax.axis_size("gy")
    number_z = lax.axis_size("gz")
    index_x = lax.axis_index("gx")
    index_y = lax.axis_index("gy")
    index_z = lax.axis_index("gz")
    terms = moment_shift.shape[1]
    padded_terms = (terms + 15) // 16 * 16
    columns = block_x * block_y
    leaves = columns * block_z
    slot_of = jnp.arange(column, dtype=jnp.int32) % SLOTS
    live_mask = (slot_of[None, None, :] < jnp.repeat(counts, SLOTS, axis=2)).astype(F32)
    weights = charges * live_mask
    stacked = jnp.concatenate([positions, weights[None]], axis=0)
    order = jnp.asarray(permutation(*sizes))
    vmem = pl.BlockSpec(memory_space=pltpu.VMEM)
    smem = pl.BlockSpec(memory_space=pltpu.SMEM)
    top_count = number_x * number_y * number_z // 8
    top_sizes = (number_x // 2, number_y // 2, number_z // 2)
    shifts = offset_table()
    offsets = shifts.shape[0]
    upper_rows = (1 + top_count + 7) // 8 * 8
    at = (index_x, index_y, index_z)
    numbers = (number_x, number_y, number_z)
    picked = 0
    admitted = True
    for axis in range(3):
        picked = picked * numbers[axis] + (at[axis] + shifts[:, axis]) % numbers[axis]
        odd = at[axis] % 2
        admitted = admitted & (shifts[:, axis] >= -2 - odd) & (shifts[:, axis] <= 3 - odd)
    picked = jnp.where(admitted, picked, -1)
    entries = number_x * number_y * number_z
    static = np.full((offsets, upper_rows), -1, np.int32)
    for row in range(offsets):
        for box in range(top_count):
            spot = (
                box // (top_sizes[1] * top_sizes[2]),
                box // top_sizes[2] % top_sizes[1],
                box % top_sizes[2],
            )
            moved = [(spot[axis] + int(shifts[row, axis])) % top_sizes[axis] for axis in range(3)]
            static[row, 1 + box] = (
                entries + (moved[0] * top_sizes[1] + moved[1]) * top_sizes[2] + moved[2]
            )
    index = jnp.where(jnp.arange(upper_rows)[None, :] == 0, picked[:, None], jnp.asarray(static))
    chosen = (index[:, :, None] == jnp.arange(entries + top_count)[None, None, :]).astype(F32)
    parent = (index_x // 2 * top_sizes[1] + index_y // 2) * top_sizes[2] + index_z // 2
    octant = index_x % 2 * 4 + index_y % 2 * 2 + index_z % 2
    where = jnp.stack([parent, octant]).astype(jnp.int32)
    wide_x, wide_y = block_x + 5, block_y + 5
    half_x, half_y = block_x // 2, block_y // 2
    potential, field_out = pl.pallas_call(
        lambda *refs: field_kernel(sizes, numbers, *refs),
        out_shape=(
            jax.ShapeDtypeStruct((columns, column), F32),
            jax.ShapeDtypeStruct((3, columns, column), F32),
        ),
        in_specs=[smem, smem] + [vmem] * 10,
        out_specs=(vmem, vmem),
        scratch_shapes=[
            pltpu.VMEM((3, block_x + 2, block_y + 2, 4, column), F32),
            pltpu.VMEM((3, block_x + 4, block_y + 4, block_z, LANES), F32),
            pltpu.VMEM((3, half_x + 4, half_y + 4, block_z // 2, LANES), F32),
            pltpu.VMEM((entries * 8 + 8, LANES), F32),
            pltpu.VMEM((leaves, LANES), F32),
            pltpu.VMEM((offsets, upper_rows, 2 * LANES), F32),
            pltpu.VMEM((36, (block_x + 4) * block_y, column), F32),
            pltpu.VMEM((7, block_x + 4 + block_x, block_y + 4 + block_y, 8, LANES), F32),
            pltpu.VMEM((7, half_x + 4 + half_x, half_y + 4 + half_y, 8, LANES), F32),
            pltpu.VMEM((offsets // 2, padded_terms, 2 * LANES), BF16),
            pltpu.VMEM((upper_rows, terms), F32),
            pltpu.VMEM(((padded_terms + 1) * columns, column), F32),
            pltpu.VMEM((columns * 8 + half_x * half_y * 8 + 2 * upper_rows, padded_terms), F32),
            pltpu.SemaphoreType.DMA((3, 27)),
            pltpu.SemaphoreType.DMA((3, 27)),
            pltpu.SemaphoreType.DMA((entries,)),
            pltpu.SemaphoreType.DMA((entries,)),
        ],
        compiler_params=pltpu.CompilerParams(
            vmem_limit_bytes=60 * 1024 * 1024, collective_id=0, has_side_effects=True
        ),
        name="fields",
    )(
        jnp.asarray(plan_table(block_x, block_y)),
        where,
        jnp.transpose(stacked, (1, 2, 0, 3)),
        stacked.reshape(4, columns, column),
        live_mask.reshape(columns, column),
        moment_shift,
        far_operators,
        local_shift,
        lattice_operator,
        order,
        jnp.asarray(permutation(*numbers)),
        chosen,
    )
    return (
        potential.reshape(block_x, block_y, column),
        field_out.reshape(3, block_x, block_y, column),
    )


def solution(mesh):
    placed = (
        P(None, "gx", "gy", "gz"),
        P("gx", "gy", "gz"),
        P("gx", "gy", "gz"),
        P(),
        P(),
        P(),
        P(),
    )
    return jax.shard_map(
        per_device,
        mesh=mesh,
        in_specs=placed,
        out_specs=(P("gx", "gy", "gz"), P(None, "gx", "gy", "gz")),
        check_vma=False,
    )
```
